128 devices in a mesh: tok: 4 (over z_lo, core), con: 4 (over x), out: 8 (over z_hi, y).
Axes of the slice: x: 4, y: 4, z: 4 (z_hi: 2, z_lo: 2; z = z_hi * 2 + z_lo), core: 2. Of those that a mesh axis runs over, the one named last changes fastest.
Arguments:
- tokens: bfloat16 [1024, 10240], P('tok', 'con'), may hold values from -6 to 6
- out_grad: bfloat16 [1024, 10240], P('tok', 'con'), may hold values from -3 to 3
- weight_in: bfloat16 [10240, 20480], P('con', ('tok', 'out')), may hold values from -0.0625 to 0.0625
- weight_out: bfloat16 [20480, 10240], P(('tok', 'out'), 'con'), may hold values from -0.0390625 to 0.0390625
Outputs:
- input_grad: bfloat16 [1024, 10240], P(('tok', 'out'), 'con')
- first_grad: float32 [10240, 20480], P('con', ('tok', 'out'))
- second_grad: float32 [20480, 10240], P(('tok', 'out'), 'con')
The draws below stay inside these ranges and needn't reach their ends.
All inputs are finite; a program needn't handle non-finite values.
Results may differ from the reference program's by a relative error of at most 0.0049.
Values may be sent and summed in bfloat16 or wider, within the bound.
No kernel may reach another device: no remote copies, remote signals or barrier semaphores. Data moves between devices by JAX's collectives and lax.ppermute only.
A program may use at most 128 MiB of HBM per device.

```python
import jax
import jax.numpy as jnp
from jax import lax

D = 10240
FF = 20480
TOKENS = 1024


def block_levels(key, dims, cuts, least, largest):
    gain, own = 1.0, jax.random.fold_in(key, 6)
    for dim, blocks in cuts:
        steps = jnp.exp(jax.random.uniform(jax.random.fold_in(own, dim), (blocks,), jnp.float32, least / len(cuts), largest / len(cuts)))
        gain = gain * jnp.repeat(steps, dims[dim] // blocks).reshape([-1 if axis == dim else 1 for axis in range(len(dims))])
    return gain


def normal_values(key, shape, spread, most, pieces=(), kind=jnp.bfloat16):
    drawn = spread * jax.random.normal(key, shape, jnp.float32)
    if pieces:
        drawn = drawn * block_levels(key, shape, pieces, -0.22, 0.18)
    return jnp.clip(drawn, -most, most).astype(kind)


def setup_inputs(seed: int = 0) -> dict:
    arg_keys = jax.random.split(jax.random.key(seed), 5)
    tokens = normal_values(arg_keys[0], (TOKENS, D), 1.0, 6.0, ((0, 4), (1, 4)))
    out_grad = normal_values(arg_keys[1], (TOKENS, D), 0.3, 3.0, ((0, 4), (1, 4)))
    weight_in = normal_values(arg_keys[2], (D, FF), D ** -0.5, 0.0625, ((0, 4), (1, 32)))
    weight_out = normal_values(arg_keys[3], (FF, D), FF ** -0.5, 0.0390625, ((0, 32), (1, 4)))
    return {"tokens": tokens, "out_grad": out_grad, "weight_in": weight_in, "weight_out": weight_out}


def gelu_parts(pre, act_grad):
    cdf = 0.5 * (1.0 + jax.scipy.special.erf(pre * 0.7071067811865476))
    density = jnp.exp(-0.5 * pre * pre) * 0.3989422804014327
    activ = (pre * cdf).astype(jnp.bfloat16)
    pre_grad = (act_grad * (cdf + pre * density)).astype(jnp.bfloat16)
    return activ, pre_grad


def reference(tokens, out_grad, weight_in, weight_out):
    pre = jnp.dot(tokens, weight_in, preferred_element_type=jnp.float32)
    act_grad = lax.dot_general(out_grad, weight_out, (((1,), (1,)), ((), ())), preferred_element_type=jnp.float32)
    activ, pre_grad = gelu_parts(pre, act_grad)
    input_grad = lax.dot_general(pre_grad, weight_in, (((1,), (1,)), ((), ())), preferred_element_type=jnp.float32)
    first_grad = lax.dot_general(tokens, pre_grad, (((0,), (0,)), ((), ())), preferred_element_type=jnp.float32)
    second_grad = lax.dot_general(activ, out_grad, (((0,), (0,)), ((), ())), preferred_element_type=jnp.float32)
    return input_grad.astype(jnp.bfloat16), first_grad, second_grad
```

```python
import jax
import jax.numpy as jnp
from jax import lax
from jax.experimental import pallas as pl
from jax.experimental.pallas import tpu as pltpu
from jax.sharding import PartitionSpec as P

INTERPRET = False
AXES = ("tok", "con", "out")
BF, F32 = jnp.bfloat16, jnp.float32


def index_of(x, y, z, k):
    return (((z % 2) * 2 + k) * 4 + x) * 8 + (z // 2) * 4 + y


def shift(v, x=0, y=0, z=0, k=0):
    r = range(4)
    pairs = [
        (index_of(a, b, c, d), index_of((a + x) % 4, (b + y) % 4, (c + z) % 4, (d + k) % 2))
        for a in r for b in r for c in r for d in range(2)
    ]
    return lax.ppermute(v, AXES, pairs)


def gelu_parts(pre, act_grad):
    cdf = 0.5 * (1.0 + jax.scipy.special.erf(pre * 0.7071067811865476))
    density = jnp.exp(-0.5 * pre * pre) * 0.3989422804014327
    activ = (pre * cdf).astype(BF)
    pre_grad = (act_grad * (cdf + pre * density)).astype(BF)
    return (activ, pre_grad)


def run(body, outs, scal, args, scratch=(), flops=0, room=4 << 20):
    vmem = pl.BlockSpec(memory_space=pltpu.VMEM)
    shapes = [jax.ShapeDtypeStruct(*o) for o in outs]
    nbytes = sum(v.size * v.dtype.itemsize for v in [*args, *shapes])
    return pl.pallas_call(
        body,
        in_specs=[pl.BlockSpec(memory_space=pltpu.SMEM)] + [vmem] * len(args),
        out_specs=[vmem] * len(outs),
        out_shape=shapes,
        scratch_shapes=list(scratch),
        cost_estimate=pl.CostEstimate(flops=flops, bytes_accessed=nbytes, transcendentals=0),
        compiler_params=pltpu.CompilerParams(vmem_limit_bytes=nbytes + room),
        interpret=INTERPRET,
    )(scal, *args)


def product(a, b, ca, cb):
    return lax.dot_general(a, b, (((ca,), (cb,)), ((), ())), preferred_element_type=F32)


def cat(refs):
    return refs[0][...] if len(refs) == 1 else jnp.concatenate([r[...] for r in refs], axis=0)


def project(scal, jobs):
    args, flops = [], 0
    for blocks, w, _ in jobs:
        args += [*blocks, w]
        flops += 2 * sum(v.shape[0] for v in blocks) * w.size
    rows = sum(v.shape[0] for v in jobs[0][0])
    hidden = jobs[0][1].shape[1 - jobs[0][2]]
    quarter = rows // 8

    def body(s, *refs):
        x = s[0]
        outs, keep, part = refs[-5:-2], refs[-2], refs[-1]
        at = 0
        for a, (blocks, _, dim) in enumerate(jobs):
            lhs = cat(refs[at : at + len(blocks)])
            w = refs[at + len(blocks)]
            at += len(blocks) + 1
            part[...] = product(lhs, w[...], 1, dim)
            for b in range(2):
                for o, j in zip(outs, (1, 3, 2)):
                    o[a, b] = part[pl.ds(b * 4 * quarter + lax.rem(x + j, 4) * quarter, quarter), :].astype(BF)
                keep[a, b] = part[pl.ds(b * 4 * quarter + x * quarter, quarter), :]

    shape = (len(jobs), 2, quarter, hidden)
    *sent, keep = run(
        body, [(shape, BF)] * 3 + [(shape, F32)], scal, args, [pltpu.VMEM((rows, hidden), F32)], flops, 12 << 20)
    return sent, keep


def back(scal, parts, pick, w):
    width = w.shape[0]
    quarter, hidden = parts[0].shape[-2:]
    tile = 512 if width % 512 == 0 else 128

    def body(s, p0, p1, p2, p3, w_ref, other, mine):
        x = s[0]
        lhs = jnp.concatenate([pick(p)[b] for b in range(2) for p in (p0, p1, p2, p3)], axis=0)
        for t in range(0, width, tile):
            res = product(lhs, w_ref[t : t + tile, :], 1, 1)
            for j in range(4):
                at = pl.ds(lax.rem(x + 4 - j, 4) * quarter, quarter)
                mine[at, t : t + tile] = res[j * quarter : (j + 1) * quarter]
                other[at, t : t + tile] = res[(4 + j) * quarter : (5 + j) * quarter].astype(BF)

    return run(
        body, [((4 * quarter, width), BF), ((4 * quarter, width), F32)], scal, [*parts, w],
        flops=16 * quarter * hidden * width, room=8 << 20)


def weight_grad(scal, lefts, rights, pick, tile_left):
    blocks, parts = (lefts, rights) if tile_left else (rights, lefts)
    width = blocks[0].shape[1]
    quarter, hidden = parts[0].shape[-2:]
    tile = 512 if width % 512 == 0 else 128
    rows = sum(v.shape[0] for v in blocks)

    def body(s, *refs):
        x = s[0]
        wide, quarters, out, held = refs[: len(blocks)], refs[len(blocks) : -2], refs[-2], refs[-1]

        @pl.when(pl.program_id(0) == 0)
        def _():
            for c, j, b in [(c, j, b) for c in range(2) for j in range(4) for b in range(2)]:
                at = pl.ds((2 * c + b) * 4 * quarter + lax.rem(x + 4 - j, 4) * quarter, quarter)
                held[at, :] = pick(quarters, c, j)[b]

        a, b = cat(wide), held[...]
        out[...] = product(a, b, 0, 0) if tile_left else product(b, a, 0, 0)

    shape = (width, hidden) if tile_left else (hidden, width)
    block = (tile, hidden) if tile_left else (hidden, tile)
    return pl.pallas_call(
        body,
        grid=(width // tile,),
        in_specs=[pl.BlockSpec(memory_space=pltpu.SMEM)]
        + [pl.BlockSpec((v.shape[0], tile), lambda i: (0, i)) for v in blocks]
        + [pl.BlockSpec(v.shape, lambda i, n=v.ndim: (0,) * n) for v in parts],
        out_specs=pl.BlockSpec(block, (lambda i: (i, 0)) if tile_left else (lambda i: (0, i))),
        out_shape=jax.ShapeDtypeStruct(shape, F32),
        scratch_shapes=[pltpu.VMEM((rows, hidden), BF)],
        cost_estimate=pl.CostEstimate(
            flops=2 * rows * width * hidden, bytes_accessed=2 * rows * (width + hidden) + 4 * width * hidden,
            transcendentals=0),
        compiler_params=pltpu.CompilerParams(vmem_limit_bytes=20 << 20),
        interpret=INTERPRET,
    )(scal, *blocks, *parts)


def f32(v):
    return v.astype(F32)


def gelu(scal, own, got, picks, before=None):
    shape = own[0].shape[1:]

    def body(s, *refs):
        n = len(own)
        keep, pieces, (activ, pre_grad) = refs[:n], refs[n : n + len(got)], refs[-2:]
        both = []
        for src, at in picks:
            p = pieces[3 * src : 3 * src + 3]
            both.append(keep[src][at] + (f32(p[0][at]) + f32(p[1][at]) + f32(p[2][at])))
        if before is None:
            activ[...], pre_grad[...] = gelu_parts(*both)
        else:
            activ[0] = refs[-3][...]
            activ[1], pre_grad[...] = gelu_parts(*both)

    more = [] if before is None else [before]
    return run(body, [((2,) * len(more) + shape, BF), (shape, BF)], scal, [*own, *got, *more])


def cut(scal, v):
    n = v.shape[0] // 2

    def body(s, v, a, b):
        a[...] = v[:n]
        b[...] = v[n:]

    return run(body, [((n, v.shape[1]), BF)] * 2, scal, [v], room=1 << 20)


def body_of(tokens, out_grad, weight_in, weight_out):
    ix = lax.axis_index("con")
    it, io = lax.axis_index("tok"), lax.axis_index("out")
    zl, zh, iy = it >> 1, io >> 2, io & 3
    scal = jnp.stack([ix, iy, zh, zh ^ zl]).astype(jnp.int32)
    rows, width = tokens.shape
    half, small = width // 2, rows // 8
    whole = lambda v: v[...]

    def around(sent, name):
        return [shift(v, **{name: j}) for v, j in zip(sent, (1, 3, 2))]

    def spread(v):
        return [v] + [shift(v, x=j) for j in (1, 2, 3)]

    partner, top = [], []
    for v in (tokens, out_grad):
        partner.append(shift(v, k=1))
        up, down = cut(scal, v)
        top.append([shift(up, z=3), shift(down, z=1)])
    sent_l, keep_l = project(
        scal, [((tokens, partner[0]), weight_in, 0), ((out_grad, partner[1]), weight_out, 1)])
    got_l = around(sent_l, "x")
    far_t = top[0] + [shift(v, k=1) for v in top[0]]
    sent_r, keep_r = project(scal, [(far_t, weight_in, 0)])
    got_r = around(sent_r, "x")
    ac_l, pg_l = gelu(scal, [keep_l], got_l, ((0, 0), (0, 1)))
    pg_l = spread(pg_l)

    far_g = top[1] + [shift(v, k=1) for v in top[1]]
    sent_g, keep_g = project(scal, [(far_g, weight_out, 1)])
    got_g = around(sent_g, "x")

    other_l, mine_l = back(scal, pg_l, whole, weight_in)
    swapped_l = shift(other_l, k=1)
    activ_q, pre_grad_q = gelu(scal, [keep_r, keep_g], [*got_r, *got_g], ((0, 0), (1, 0)), ac_l)
    pg_r = spread(pre_grad_q)
    activ = spread(activ_q)

    def mid_l(s, mine, got, send, keep):
        n = 4 * small
        a, b = pl.ds(s[2] * n, n), pl.ds((1 - s[2]) * n, n)
        keep[...] = mine[a, :] + f32(got[a, :])
        send[...] = (mine[b, :] + f32(got[b, :])).astype(BF)

    send, keep = run(
        mid_l, [((4 * small, width), BF), ((4 * small, width), F32)], scal, [mine_l, swapped_l])
    other = shift(send, z=2)

    other_r, mine_r = back(scal, pg_r, whole, weight_in)
    swapped_r = shift(other_r, k=1)

    def mid_r(s, mine, got, o1, o3, o2, stay, up, down):
        for g in range(2):
            for o, j in ((o1, 1), (o3, 3), (o2, 2)):
                at = pl.ds((g * 4 + lax.rem(s[1] + j, 4)) * small, small)
                o[g] = (mine[at, :half] + f32(got[at, :half])).astype(BF)
            at = pl.ds((g * 4 + s[1]) * small, small)
            stay[g] = mine[at, :half] + f32(got[at, :half])
        n = 4 * small
        for o, g in ((up, s[3]), (down, 1 - s[3])):
            at = pl.ds(g * n, n)
            o[...] = (mine[at, half:] + f32(got[at, half:])).astype(BF)

    group, part = (2, small, half), (4 * small, half)
    *send, stay, up, down = run(
        mid_r, [(group, BF)] * 3 + [(group, F32)] + [(part, BF)] * 2, scal, [mine_r, swapped_r])
    got_a = around(send, "y")
    got_b = [shift(up, z=1), shift(down, z=3)]
    first_grad = weight_grad(
        scal, [tokens, partner[0], *far_t], [*pg_l, *pg_r], lambda v, c, j: v[4 * c + j], True)

    def next_r(s, stay, a1, a3, a2, b0, b1, kept, got, up, down, o1, o3, o2, own):
        for o, g in ((up, s[3]), (down, 1 - s[3])):
            o[...] = (stay[g] + (f32(a1[g]) + f32(a3[g]) + f32(a2[g]))).astype(BF)
        for o, j in ((o1, 1), (o3, 3), (o2, 2), (own, 0)):
            at = pl.ds(lax.rem(s[1] + j, 4) * small, small)
            v = kept[at, :] + f32(got[at, :])
            o[:, :half] = v[:, :half].astype(o.dtype)
            o[:, half:] = (v[:, half:] + (f32(b0[at, :]) + f32(b1[at, :]))).astype(o.dtype)

    up, down, *send, own = run(
        next_r, [((small, half), BF)] * 2 + [((small, width), BF)] * 3 + [((small, width), F32)], scal,
        [stay, *got_a, *got_b, keep, other])
    got_a = [shift(up, z=1), shift(down, z=3)]
    got_b = around(send, "y")
    second_grad = weight_grad(
        scal, activ, [out_grad, partner[1], *far_g], lambda v, c, j: v[j].at[c], False)

    def last(s, own, b1, b3, b2, a0, a1, out):
        v = own[...] + (f32(b1[...]) + f32(b3[...]) + f32(b2[...]))
        out[:, :half] = (v[:, :half] + (f32(a0[...]) + f32(a1[...]))).astype(BF)
        out[:, half:] = v[:, half:].astype(BF)

    (input_grad,) = run(last, [((small, width), BF)], scal, [own, *got_b, *got_a])
    return (input_grad, first_grad, second_grad)


def solution(mesh):
    placed = (P("tok", "con"), P("tok", "con"), P("con", ("tok", "out")), P(("tok", "out"), "con"))
    return jax.shard_map(
        body_of,
        mesh=mesh,
        in_specs=placed,
        out_specs=(P(("tok", "out"), "con"), P("con", ("tok", "out")), P(("tok", "out"), "con")),
        check_vma=False,
    )
```

```python
import jax
import jax.numpy as jnp
from jax import lax
from jax.experimental import pallas as pl
from jax.experimental.pallas import tpu as pltpu
from jax.sharding import PartitionSpec as P

INTERPRET = False
WARM = 30_000_000_000
FIRST_TILE, SECOND_TILE = 1280, 1280
AXES = ("tok", "con", "out")
BF, F32 = jnp.bfloat16, jnp.float32


def index_of(x, y, z, k):
    return (((z % 2) * 2 + k) * 4 + x) * 8 + (z // 2) * 4 + y


def shift(v, x=0, y=0, z=(0, 0), k=0):
    r = range(4)
    pairs = [
        (index_of(a, b, c, d), index_of((a + x) % 4, (b + y) % 4, (c + z[d]) % 4, (d + k) % 2))
        for a in r for b in r for c in r for d in range(2)
    ]
    return lax.ppermute(v, AXES, pairs)


def gelu_parts(pre, act_grad):
    cdf = 0.5 * (1.0 + jax.scipy.special.erf(pre * 0.7071067811865476))
    density = jnp.exp(-0.5 * pre * pre) * 0.3989422804014327
    activ = (pre * cdf).astype(BF)
    pre_grad = (act_grad * (cdf + pre * density)).astype(BF)
    return (activ, pre_grad)


def run(body, outs, scal, args, scratch=(), flops=0, room=4 << 20):
    vmem = pl.BlockSpec(memory_space=pltpu.VMEM)
    shapes = [jax.ShapeDtypeStruct(*o) for o in outs]
    nbytes = sum(v.size * v.dtype.itemsize for v in [*args, *shapes])
    return pl.pallas_call(
        body,
        in_specs=[pl.BlockSpec(memory_space=pltpu.SMEM)] + [vmem] * len(args),
        out_specs=[vmem] * len(outs),
        out_shape=shapes,
        scratch_shapes=list(scratch),
        cost_estimate=pl.CostEstimate(flops=flops, bytes_accessed=nbytes, transcendentals=0),
        compiler_params=pltpu.CompilerParams(vmem_limit_bytes=nbytes + room),
        interpret=INTERPRET,
    )(scal, *args)


def product(a, b, ca, cb):
    return lax.dot_general(a, b, (((ca,), (cb,)), ((), ())), preferred_element_type=F32)


def cat(refs):
    return refs[0][...] if len(refs) == 1 else jnp.concatenate([r[...] for r in refs], axis=0)


def project(scal, jobs):
    args, flops = [], 0
    for blocks, w, _ in jobs:
        args += [*blocks, w]
        flops += 2 * sum(v.shape[0] for v in blocks) * w.size
    rows = sum(v.shape[0] for v in jobs[0][0])
    hidden = jobs[0][1].shape[1 - jobs[0][2]]
    quarter = rows // 8

    def body(s, *refs):
        x = s[0]
        outs, keep, part = refs[-5:-2], refs[-2], refs[-1]
        at = 0
        for a, (blocks, _, dim) in enumerate(jobs):
            lhs = cat(refs[at : at + len(blocks)])
            w = refs[at + len(blocks)]
            at += len(blocks) + 1
            part[...] = product(lhs, w[...], 1, dim)
            for b in range(2):
                for o, j in zip(outs, (1, 3, 2)):
                    o[a, b] = part[pl.ds(b * 4 * quarter + lax.rem(x + j, 4) * quarter, quarter), :].astype(BF)
                keep[a, b] = part[pl.ds(b * 4 * quarter + x * quarter, quarter), :]

    shape = (len(jobs), 2, quarter, hidden)
    *sent, keep = run(
        body, [(shape, BF)] * 3 + [(shape, F32)], scal, args, [pltpu.VMEM((rows, hidden), F32)], flops, 12 << 20)
    return sent, keep


def warm(scal):
    def body(s, o):
        for i in range(scal.shape[0]):
            o[i] = s[i]

    smem = pl.BlockSpec(memory_space=pltpu.SMEM)
    return pl.pallas_call(
        body,
        in_specs=[smem],
        out_specs=smem,
        out_shape=jax.ShapeDtypeStruct(scal.shape, scal.dtype),
        cost_estimate=pl.CostEstimate(flops=WARM, bytes_accessed=32, transcendentals=0),
        compiler_params=pltpu.CompilerParams(vmem_limit_bytes=1 << 20),
        interpret=INTERPRET,
    )(scal)


def project_block(scal, rows, w, dim, prior=None):
    hidden = w.shape[1 - dim]
    quarter = rows.shape[0] // 4
    last = prior is not None

    def body(s, v, w, *refs):
        outs, part = refs[-5:-1], refs[-1]
        part[...] = product(v[...], w[...], 1, dim)
        for i, (o, j) in enumerate(zip(outs, (1, 3, 2, 0))):
            new = part[pl.ds(lax.rem(s[0] + j, 4) * quarter, quarter), :].astype(o.dtype)
            if last:
                o[0, 0] = refs[i][...]
                o[0, 1] = new
            else:
                o[...] = new

    shape = (1, 2, quarter, hidden) if last else (quarter, hidden)
    return run(
        body, [(shape, BF)] * 3 + [(shape, F32)], scal, [rows, w, *(prior or [])],
        [pltpu.VMEM((4 * quarter, hidden), F32)], 2 * rows.shape[0] * w.size, 6 << 20)


def back(scal, parts, b, w, kind):
    width = w.shape[0]
    quarter, hidden = parts[0].shape[-2:]
    tile = 512 if width % 512 == 0 else 128

    def body(s, p0, p1, p2, p3, w_ref, out):
        lhs = jnp.concatenate([p[b] for p in (p0, p1, p2, p3)], axis=0)
        for t in range(0, width, tile):
            res = product(lhs, w_ref[t : t + tile, :], 1, 1)
            for j in range(4):
                at = pl.ds(lax.rem(s[0] + 4 - j, 4) * quarter, quarter)
                out[at, t : t + tile] = res[j * quarter : (j + 1) * quarter].astype(kind)

    (out,) = run(
        body, [((4 * quarter, width), kind)], scal, [*parts, w],
        flops=8 * quarter * hidden * width, room=6 << 20)
    return out


def weight_grad(scal, lefts, rights, pick, tile_left):
    blocks, parts = (lefts, rights) if tile_left else (rights, lefts)
    width = blocks[0].shape[1]
    quarter, hidden = parts[0].shape[-2:]
    wanted = FIRST_TILE if tile_left else SECOND_TILE
    tile = wanted if width % wanted == 0 else 128
    rows = sum(v.shape[0] for v in blocks)

    def body(s, *refs):
        x = s[0]
        wide, quarters, out, held = refs[: len(blocks)], refs[len(blocks) : -2], refs[-2], refs[-1]

        @pl.when(pl.program_id(0) == 0)
        def _():
            for c, j, b in [(c, j, b) for c in range(2) for j in range(4) for b in range(2)]:
                at = pl.ds((2 * c + b) * 4 * quarter + lax.rem(x + 4 - j, 4) * quarter, quarter)
                held[at, :] = pick(quarters, c, j)[b]

        a, b = cat(wide), held[...]
        out[...] = product(a, b, 0, 0) if tile_left else product(b, a, 0, 0)

    shape = (width, hidden) if tile_left else (hidden, width)
    block = (tile, hidden) if tile_left else (hidden, tile)
    return pl.pallas_call(
        body,
        grid=(width // tile,),
        in_specs=[pl.BlockSpec(memory_space=pltpu.SMEM)]
        + [pl.BlockSpec((v.shape[0], tile), lambda i: (0, i)) for v in blocks]
        + [pl.BlockSpec(v.shape, lambda i, n=v.ndim: (0,) * n) for v in parts],
        out_specs=pl.BlockSpec(block, (lambda i: (i, 0)) if tile_left else (lambda i: (0, i))),
        out_shape=jax.ShapeDtypeStruct(shape, F32),
        scratch_shapes=[pltpu.VMEM((rows, hidden), BF)],
        cost_estimate=pl.CostEstimate(
            flops=2 * rows * width * hidden, bytes_accessed=2 * rows * (width + hidden) + 4 * width * hidden,
            transcendentals=0),
        compiler_params=pltpu.CompilerParams(vmem_limit_bytes=30 << 20),
        interpret=INTERPRET,
    )(scal, *blocks, *parts)


def f32(v):
    return v.astype(F32)


def gelu(scal, own, got, picks, before=None):
    shape = own[0].shape[1:]

    def body(s, *refs):
        n = len(own)
        keep, pieces, (activ, pre_grad) = refs[:n], refs[n : n + len(got)], refs[-2:]
        both = []
        for src, at in picks:
            p = pieces[3 * src : 3 * src + 3]
            both.append(keep[src][at] + (f32(p[0][at]) + f32(p[1][at]) + f32(p[2][at])))
        if before is None:
            activ[...], pre_grad[...] = gelu_parts(*both)
        else:
            activ[0] = refs[-3][...]
            activ[1], pre_grad[...] = gelu_parts(*both)

    more = [] if before is None else [before]
    return run(body, [((2,) * len(more) + shape, BF), (shape, BF)], scal, [*own, *got, *more])


def body_of(tokens, out_grad, weight_in, weight_out):
    ix = lax.axis_index("con")
    it, io = lax.axis_index("tok"), lax.axis_index("out")
    zl, zh, iy = it >> 1, io >> 2, io & 3
    scal = jnp.stack([ix, iy, zh, zh ^ zl]).astype(jnp.int32)
    scal = warm(scal)
    rows, width = tokens.shape
    half, small = width // 2, rows // 8

    def around(sent, name):
        return [shift(v, **{name: j}) for v, j in zip(sent, (1, 3, 2))]

    def spread(v):
        return [v] + [shift(v, x=j) for j in (1, 2, 3)]

    partner, far = [], []
    for v in (tokens, out_grad):
        partner.append(shift(v, k=1))
        far.append(shift(v, z=(3, 1)))
    sent_l, keep_l = project(
        scal, [((tokens, partner[0]), weight_in, 0), ((out_grad, partner[1]), weight_out, 1)])
    got_l = around(sent_l, "x")
    far_t = [far[0], shift(far[0], k=1)]
    prior = project_block(scal, far_t[0], weight_in, 0)
    *sent_r, keep_r = project_block(scal, far_t[1], weight_in, 0, prior)
    got_r = around(sent_r, "x")
    ac_l, pg_l = gelu(scal, [keep_l], got_l, ((0, 0), (0, 1)))
    pg_l = spread(pg_l)

    far_g = [far[1], shift(far[1], k=1)]
    prior = project_block(scal, far_g[0], weight_out, 1)
    *sent_g, keep_g = project_block(scal, far_g[1], weight_out, 1, prior)
    got_g = around(sent_g, "x")

    swapped_l = shift(back(scal, pg_l, 1, weight_in, BF), k=1)
    mine_l = back(scal, pg_l, 0, weight_in, F32)
    activ_q, pre_grad_q = gelu(scal, [keep_r, keep_g], [*got_r, *got_g], ((0, 0), (1, 0)), ac_l)
    pg_r = spread(pre_grad_q)
    activ = spread(activ_q)

    def mid_l(s, mine, got, send, keep):
        n = 4 * small
        a, b = pl.ds(s[2] * n, n), pl.ds((1 - s[2]) * n, n)
        keep[...] = mine[a, :] + f32(got[a, :])
        send[...] = (mine[b, :] + f32(got[b, :])).astype(BF)

    send, keep = run(
        mid_l, [((4 * small, width), BF), ((4 * small, width), F32)], scal, [mine_l, swapped_l])
    other = shift(send, z=(2, 2))

    swapped_r = shift(back(scal, pg_r, 1, weight_in, BF), k=1)
    mine_r = back(scal, pg_r, 0, weight_in, F32)

    def mid_r(s, mine, got, o1, o3, o2, stay, up, down):
        for g in range(2):
            for o, j in ((o1, 1), (o3, 3), (o2, 2)):
                at = pl.ds((g * 4 + lax.rem(s[1] + j, 4)) * small, small)
                o[g] = (mine[at, :half] + f32(got[at, :half])).astype(BF)
            at = pl.ds((g * 4 + s[1]) * small, small)
            stay[g] = mine[at, :half] + f32(got[at, :half])
        n = 4 * small
        for o, g in ((up, s[3]), (down, 1 - s[3])):
            at = pl.ds(g * n, n)
            o[...] = (mine[at, half:] + f32(got[at, half:])).astype(BF)

    group, part = (2, small, half), (4 * small, half)
    *send, stay, up, down = run(
        mid_r, [(group, BF)] * 3 + [(group, F32)] + [(part, BF)] * 2, scal, [mine_r, swapped_r])
    got_a = around(send, "y")
    got_b = [shift(up, z=(1, 1)), shift(down, z=(3, 3))]
    first_grad = weight_grad(
        scal, [tokens, partner[0], *far_t], [*pg_l, *pg_r], lambda v, c, j: v[4 * c + j], True)

    def next_r(s, stay, a1, a3, a2, b0, b1, kept, got, up, down, o1, o3, o2, own):
        for o, g in ((up, s[3]), (down, 1 - s[3])):
            o[...] = (stay[g] + (f32(a1[g]) + f32(a3[g]) + f32(a2[g]))).astype(BF)
        for o, j in ((o1, 1), (o3, 3), (o2, 2), (own, 0)):
            at = pl.ds(lax.rem(s[1] + j, 4) * small, small)
            v = kept[at, :] + f32(got[at, :])
            o[:, :half] = v[:, :half].astype(o.dtype)
            o[:, half:] = (v[:, half:] + (f32(b0[at, :]) + f32(b1[at, :]))).astype(o.dtype)

    up, down, *send, own = run(
        next_r, [((small, half), BF)] * 2 + [((small, width), BF)] * 3 + [((small, width), F32)], scal,
        [stay, *got_a, *got_b, keep, other])
    got_a = [shift(up, z=(1, 1)), shift(down, z=(3, 3))]
    got_b = around(send, "y")
    second_grad = weight_grad(
        scal, activ, [out_grad, partner[1], *far_g], lambda v, c, j: v[j].at[c], False)

    def last(s, own, b1, b3, b2, a0, a1, out):
        v = own[...] + (f32(b1[...]) + f32(b3[...]) + f32(b2[...]))
        out[:, :half] = (v[:, :half] + (f32(a0[...]) + f32(a1[...]))).astype(BF)
        out[:, half:] = v[:, half:].astype(BF)

    (input_grad,) = run(last, [((small, width), BF)], scal, [own, *got_b, *got_a])
    return (input_grad, first_grad, second_grad)


def solution(mesh):
    placed = (P("tok", "con"), P("tok", "con"), P("con", ("tok", "out")), P(("tok", "out"), "con"))
    return jax.shard_map(
        body_of,
        mesh=mesh,
        in_specs=placed,
        out_specs=(P(("tok", "out"), "con"), P("con", ("tok", "out")), P(("tok", "out"), "con")),
        check_vma=False,
    )
```

```python
import jax
import jax.numpy as jnp
from jax import lax
from jax.experimental import pallas as pl
from jax.experimental.pallas import tpu as pltpu
from jax.sharding import PartitionSpec as P

INTERPRET = False
WARM = 30_000_000_000
FIRST_TILE, SECOND_TILE = 1280, 1280
AXES = ("tok", "con", "out")
BF, F32 = jnp.bfloat16, jnp.float32


def index_of(x, y, z, k):
    return (((z % 2) * 2 + k) * 4 + x) * 8 + (z // 2) * 4 + y


def shift(v, x=0, y=0, z=(0, 0), k=0):
    r = range(4)
    pairs = [
        (index_of(a, b, c, d), index_of((a + x) % 4, (b + y) % 4, (c + z[d]) % 4, (d + k) % 2))
        for a in r for b in r for c in r for d in range(2)
    ]
    return lax.ppermute(v, AXES, pairs)


def gelu_parts(pre, act_grad):
    cdf = 0.5 * (1.0 + jax.scipy.special.erf(pre * 0.7071067811865476))
    density = jnp.exp(-0.5 * pre * pre) * 0.3989422804014327
    activ = (pre * cdf).astype(BF)
    pre_grad = (act_grad * (cdf + pre * density)).astype(BF)
    return (activ, pre_grad)


def run(body, outs, scal, args, scratch=(), flops=0, room=4 << 20):
    vmem = pl.BlockSpec(memory_space=pltpu.VMEM)
    shapes = [jax.ShapeDtypeStruct(*o) for o in outs]
    nbytes = sum(v.size * v.dtype.itemsize for v in [*args, *shapes])
    return pl.pallas_call(
        body,
        in_specs=[pl.BlockSpec(memory_space=pltpu.SMEM)] + [vmem] * len(args),
        out_specs=[vmem] * len(outs),
        out_shape=shapes,
        scratch_shapes=list(scratch),
        cost_estimate=pl.CostEstimate(flops=flops, bytes_accessed=nbytes, transcendentals=0),
        compiler_params=pltpu.CompilerParams(vmem_limit_bytes=nbytes + room),
        interpret=INTERPRET,
    )(scal, *args)


def product(a, b, ca, cb):
    return lax.dot_general(a, b, (((ca,), (cb,)), ((), ())), preferred_element_type=F32)


def cat(refs):
    return refs[0][...] if len(refs) == 1 else jnp.concatenate([r[...] for r in refs], axis=0)


def project(scal, jobs, prior=()):
    args, flops = list(prior), 0
    first = prior[0].shape[0] if prior else 0
    for blocks, w, _ in jobs:
        args += [*blocks, w]
        flops += 2 * sum(v.shape[0] for v in blocks) * w.size
    rows = sum(v.shape[0] for v in jobs[0][0])
    hidden = jobs[0][1].shape[1 - jobs[0][2]]
    quarter = rows // 8

    def body(s, *refs):
        x = s[0]
        outs, keep, part = refs[-5:-2], refs[-2], refs[-1]
        at = len(prior)
        for o, p in zip((*outs, keep), refs[:at]):
            o[:first] = p[...]
        for a, (blocks, _, dim) in enumerate(jobs, first):
            lhs = cat(refs[at : at + len(blocks)])
            w = refs[at + len(blocks)]
            at += len(blocks) + 1
            part[...] = product(lhs, w[...], 1, dim)
            for b in range(2):
                for o, j in zip(outs, (1, 3, 2)):
                    o[a, b] = part[pl.ds(b * 4 * quarter + lax.rem(x + j, 4) * quarter, quarter), :].astype(BF)
                keep[a, b] = part[pl.ds(b * 4 * quarter + x * quarter, quarter), :]

    shape = (first + len(jobs), 2, quarter, hidden)
    *sent, keep = run(
        body, [(shape, BF)] * 3 + [(shape, F32)], scal, args, [pltpu.VMEM((rows, hidden), F32)], flops, 12 << 20)
    return [*sent, keep]


def warm(scal):
    def body(s, o):
        for i in range(scal.shape[0]):
            o[i] = s[i]

    smem = pl.BlockSpec(memory_space=pltpu.SMEM)
    return pl.pallas_call(
        body,
        in_specs=[smem],
        out_specs=smem,
        out_shape=jax.ShapeDtypeStruct(scal.shape, scal.dtype),
        cost_estimate=pl.CostEstimate(flops=WARM, bytes_accessed=32, transcendentals=0),
        compiler_params=pltpu.CompilerParams(vmem_limit_bytes=1 << 20),
        interpret=INTERPRET,
    )(scal)


def project_block(scal, rows, w, dim, prior=None):
    hidden = w.shape[1 - dim]
    quarter = rows.shape[0] // 4
    last = prior is not None

    def body(s, v, w, *refs):
        outs, part = refs[-5:-1], refs[-1]
        part[...] = product(v[...], w[...], 1, dim)
        for i, (o, j) in enumerate(zip(outs, (1, 3, 2, 0))):
            new = part[pl.ds(lax.rem(s[0] + j, 4) * quarter, quarter), :].astype(o.dtype)
            if last:
                o[0, 0] = refs[i][...]
                o[0, 1] = new
            else:
                o[...] = new

    shape = (1, 2, quarter, hidden) if last else (quarter, hidden)
    return run(
        body, [(shape, BF)] * 3 + [(shape, F32)], scal, [rows, w, *(prior or [])],
        [pltpu.VMEM((4 * quarter, hidden), F32)], 2 * rows.shape[0] * w.size, 6 << 20)


def back(scal, parts, b, w, kind):
    width = w.shape[0]
    quarter, hidden = parts[0].shape[-2:]
    tile = 512 if width % 512 == 0 else 128

    def body(s, p0, p1, p2, p3, w_ref, out):
        lhs = jnp.concatenate([p[b] for p in (p0, p1, p2, p3)], axis=0)
        for t in range(0, width, tile):
            res = product(lhs, w_ref[t : t + tile, :], 1, 1)
            for j in range(4):
                at = pl.ds(lax.rem(s[0] + 4 - j, 4) * quarter, quarter)
                out[at, t : t + tile] = res[j * quarter : (j + 1) * quarter].astype(kind)

    (out,) = run(
        body, [((4 * quarter, width), kind)], scal, [*parts, w],
        flops=8 * quarter * hidden * width, room=6 << 20)
    return out


def weight_grad(scal, lefts, rights, pick, tile_left):
    blocks, parts = (lefts, rights) if tile_left else (rights, lefts)
    width = blocks[0].shape[1]
    quarter, hidden = parts[0].shape[-2:]
    wanted = FIRST_TILE if tile_left else SECOND_TILE
    tile = wanted if width % wanted == 0 else 128
    rows = sum(v.shape[0] for v in blocks)

    def body(s, *refs):
        x = s[0]
        wide, quarters, out, held = refs[: len(blocks)], refs[len(blocks) : -2], refs[-2], refs[-1]

        @pl.when(pl.program_id(0) == 0)
        def _():
            for c, j, b in [(c, j, b) for c in range(2) for j in range(4) for b in range(2)]:
                at = pl.ds((2 * c + b) * 4 * quarter + lax.rem(x + 4 - j, 4) * quarter, quarter)
                held[at, :] = pick(quarters, c, j)[b]

        a, b = cat(wide), held[...]
        out[...] = product(a, b, 0, 0) if tile_left else product(b, a, 0, 0)

    shape = (width, hidden) if tile_left else (hidden, width)
    block = (tile, hidden) if tile_left else (hidden, tile)
    return pl.pallas_call(
        body,
        grid=(width // tile,),
        in_specs=[pl.BlockSpec(memory_space=pltpu.SMEM)]
        + [pl.BlockSpec((v.shape[0], tile), lambda i: (0, i)) for v in blocks]
        + [pl.BlockSpec(v.shape, lambda i, n=v.ndim: (0,) * n) for v in parts],
        out_specs=pl.BlockSpec(block, (lambda i: (i, 0)) if tile_left else (lambda i: (0, i))),
        out_shape=jax.ShapeDtypeStruct(shape, F32),
        scratch_shapes=[pltpu.VMEM((rows, hidden), BF)],
        cost_estimate=pl.CostEstimate(
            flops=2 * rows * width * hidden, bytes_accessed=2 * rows * (width + hidden) + 4 * width * hidden,
            transcendentals=0),
        compiler_params=pltpu.CompilerParams(vmem_limit_bytes=30 << 20),
        interpret=INTERPRET,
    )(scal, *blocks, *parts)


def f32(v):
    return v.astype(F32)


def gelu(scal, own, got, picks, before=None):
    shape = own[0].shape[1:]

    def body(s, *refs):
        n = len(own)
        keep, pieces, (activ, pre_grad) = refs[:n], refs[n : n + len(got)], refs[-2:]
        both = []
        for src, at in picks:
            p = pieces[3 * src : 3 * src + 3]
            both.append(keep[src][at] + (f32(p[0][at]) + f32(p[1][at]) + f32(p[2][at])))
        if before is None:
            activ[...], pre_grad[...] = gelu_parts(*both)
        else:
            activ[0] = refs[-3][...]
            activ[1], pre_grad[...] = gelu_parts(*both)

    more = [] if before is None else [before]
    return run(body, [((2,) * len(more) + shape, BF), (shape, BF)], scal, [*own, *got, *more])


def body_of(tokens, out_grad, weight_in, weight_out):
    ix = lax.axis_index("con")
    it, io = lax.axis_index("tok"), lax.axis_index("out")
    zl, zh, iy = it >> 1, io >> 2, io & 3
    scal = jnp.stack([ix, iy, zh, zh ^ zl]).astype(jnp.int32)
    scal = warm(scal)
    rows, width = tokens.shape
    half, small = width // 2, rows // 8

    def around(sent, name):
        return [shift(v, **{name: j}) for v, j in zip(sent, (1, 3, 2))]

    def spread(v):
        return [v] + [shift(v, x=j) for j in (1, 2, 3)]

    partner, far = [], []
    for v in (tokens, out_grad):
        partner.append(shift(v, k=1))
        far.append(shift(v, z=(3, 1)))
    prior = project(scal, [((tokens, partner[0]), weight_in, 0)])
    *sent_l, keep_l = project(scal, [((out_grad, partner[1]), weight_out, 1)], prior)
    got_l = around(sent_l, "x")
    far_t = [far[0], shift(far[0], k=1)]
    prior = project_block(scal, far_t[0], weight_in, 0)
    *sent_r, keep_r = project_block(scal, far_t[1], weight_in, 0, prior)
    got_r = around(sent_r, "x")
    ac_l, pg_l = gelu(scal, [keep_l], got_l, ((0, 0), (0, 1)))
    pg_l = spread(pg_l)

    far_g = [far[1], shift(far[1], k=1)]
    prior = project_block(scal, far_g[0], weight_out, 1)
    *sent_g, keep_g = project_block(scal, far_g[1], weight_out, 1, prior)
    got_g = around(sent_g, "x")

    swapped_l = shift(back(scal, pg_l, 1, weight_in, BF), k=1)
    mine_l = back(scal, pg_l, 0, weight_in, F32)
    activ_q, pre_grad_q = gelu(scal, [keep_r, keep_g], [*got_r, *got_g], ((0, 0), (1, 0)), ac_l)
    pg_r = spread(pre_grad_q)
    activ = spread(activ_q)

    def mid_l(s, mine, got, send, keep):
        n = 4 * small
        a, b = pl.ds(s[2] * n, n), pl.ds((1 - s[2]) * n, n)
        keep[...] = mine[a, :] + f32(got[a, :])
        send[...] = (mine[b, :] + f32(got[b, :])).astype(BF)

    send, keep = run(
        mid_l, [((4 * small, width), BF), ((4 * small, width), F32)], scal, [mine_l, swapped_l])
    other = shift(send, z=(2, 2))

    swapped_r = shift(back(scal, pg_r, 1, weight_in, BF), k=1)
    mine_r = back(scal, pg_r, 0, weight_in, F32)

    def mid_r(s, mine, got, o1, o3, o2, stay, up, down):
        for g in range(2):
            for o, j in ((o1, 1), (o3, 3), (o2, 2)):
                at = pl.ds((g * 4 + lax.rem(s[1] + j, 4)) * small, small)
                o[g] = (mine[at, :half] + f32(got[at, :half])).astype(BF)
            at = pl.ds((g * 4 + s[1]) * small, small)
            stay[g] = mine[at, :half] + f32(got[at, :half])
        n = 4 * small
        for o, g in ((up, s[3]), (down, 1 - s[3])):
            at = pl.ds(g * n, n)
            o[...] = (mine[at, half:] + f32(got[at, half:])).astype(BF)

    group, part = (2, small, half), (4 * small, half)
    *send, stay, up, down = run(
        mid_r, [(group, BF)] * 3 + [(group, F32)] + [(part, BF)] * 2, scal, [mine_r, swapped_r])
    got_a = around(send, "y")
    got_b = [shift(up, z=(1, 1)), shift(down, z=(3, 3))]
    first_grad = weight_grad(
        scal, [tokens, partner[0], *far_t], [*pg_l, *pg_r], lambda v, c, j: v[4 * c + j], True)

    def next_r(s, stay, a1, a3, a2, b0, b1, kept, got, up, down, o1, o3, o2, own):
        for o, g in ((up, s[3]), (down, 1 - s[3])):
            o[...] = (stay[g] + (f32(a1[g]) + f32(a3[g]) + f32(a2[g]))).astype(BF)
        for o, j in ((o1, 1), (o3, 3), (o2, 2), (own, 0)):
            at = pl.ds(lax.rem(s[1] + j, 4) * small, small)
            v = kept[at, :] + f32(got[at, :])
            o[:, :half] = v[:, :half].astype(o.dtype)
            o[:, half:] = (v[:, half:] + (f32(b0[at, :]) + f32(b1[at, :]))).astype(o.dtype)

    up, down, *send, own = run(
        next_r, [((small, half), BF)] * 2 + [((small, width), BF)] * 3 + [((small, width), F32)], scal,
        [stay, *got_a, *got_b, keep, other])
    got_a = [shift(up, z=(1, 1)), shift(down, z=(3, 3))]
    got_b = around(send, "y")
    second_grad = weight_grad(
        scal, activ, [out_grad, partner[1], *far_g], lambda v, c, j: v[j].at[c], False)

    def last(s, own, b1, b3, b2, a0, a1, out):
        v = own[...] + (f32(b1[...]) + f32(b3[...]) + f32(b2[...]))
        out[:, :half] = (v[:, :half] + (f32(a0[...]) + f32(a1[...]))).astype(BF)
        out[:, half:] = v[:, half:].astype(BF)

    (input_grad,) = run(last, [((small, width), BF)], scal, [own, *got_b, *got_a])
    return (input_grad, first_grad, second_grad)


def solution(mesh):
    placed = (P("tok", "con"), P("tok", "con"), P("con", ("tok", "out")), P(("tok", "out"), "con"))
    return jax.shard_map(
        body_of,
        mesh=mesh,
        in_specs=placed,
        out_specs=(P(("tok", "out"), "con"), P("con", ("tok", "out")), P(("tok", "out"), "con")),
        check_vma=False,
    )
```
